32 devices in a mesh: section: 2 (over y), fsdp: 4 (over z), replica: 4 (over x, core).
Axes of the slice: x: 2, y: 2, z: 4, core: 2. Of those that a mesh axis runs over, the one named last changes fastest.
Arguments:
- latents: float32 [32, 256, 384], P(('fsdp', 'replica')), may hold values from -60 to 60
- condition: float32 [32, 384], P(('fsdp', 'replica')), may hold values from -5 to 5
- cotangent: float32 [32, 256, 384], P(('fsdp', 'replica')), may hold values from -5 to 5
- w_ada: bfloat16 [2, 384, 2304], P('section', 'fsdp'), may hold values from -0.3125 to 0.3125
- b_ada: bfloat16 [2, 2304], P('section', 'fsdp'), may hold values from -3 to 3
- w_qkv: bfloat16 [2, 384, 1152], P('section', 'fsdp'), may hold values from -0.20412415 to 0.20412415
- b_qv: bfloat16 [2, 768], P('section', 'fsdp'), may hold values from -3 to 3
- w_proj: bfloat16 [2, 384, 384], P('section', 'fsdp'), may hold values from -1.25 to 1.25
- b_proj: bfloat16 [2, 384], P('section', 'fsdp'), may hold values from -3 to 3
- w_fc1: bfloat16 [2, 384, 1536], P('section', 'fsdp'), may hold values from -0.3125 to 0.3125
- b_fc1: bfloat16 [2, 1536], P('section', 'fsdp'), may hold values from -3 to 3
- w_fc2: bfloat16 [2, 1536, 384], P('section', 'fsdp'), may hold values from -0.15625 to 0.15625
- b_fc2: bfloat16 [2, 384], P('section', 'fsdp'), may hold values from -3 to 3
Outputs:
- section_out: float32 [2, 32, 256, 384], P('section', ('fsdp', 'replica'))
- input_grads: float32 [2, 32, 256, 384], P('section', ('fsdp', 'replica'))
- cond_grad: float32 [32, 384], P(('fsdp', 'replica'))
- grad_w_ada: float32 [2, 384, 2304], P('section', 'fsdp')
- grad_b_ada: float32 [2, 2304], P('section', 'fsdp')
- grad_w_qkv: float32 [2, 384, 1152], P('section', 'fsdp')
- grad_b_qv: float32 [2, 768], P('section', 'fsdp')
- grad_w_proj: float32 [2, 384, 384], P('section', 'fsdp')
- grad_b_proj: float32 [2, 384], P('section', 'fsdp')
- grad_w_fc1: float32 [2, 384, 1536], P('section', 'fsdp')
- grad_b_fc1: float32 [2, 1536], P('section', 'fsdp')
- grad_w_fc2: float32 [2, 1536, 384], P('section', 'fsdp')
- grad_b_fc2: float32 [2, 384], P('section', 'fsdp')
The draws below stay inside these ranges and needn't reach their ends.
All inputs are finite; a program needn't handle non-finite values.
Results may differ from the reference program's by a relative error of at most 0.035.
Values may be sent and summed in bfloat16 or wider, within the bound.
No kernel may reach another device: no remote copies, remote signals or barrier semaphores. Data moves between devices by JAX's collectives and lax.ppermute only.
A program may use at most 128 MiB of HBM per device.

```python
import math
import jax
import jax.numpy as jnp
from jax import lax

HEADS = 6
HEAD_DIM = 64
D = 384
FF = 1536
MOD = 2304
LEN = 256
LAYERS = 2
SEQS = 32


def draw_latents(key, part):
    base_key, row_key, column_key = jax.random.split(key, 3)
    base_rows = jnp.clip(jax.random.normal(base_key, (SEQS, LEN, D), jnp.float32), -4.0, 4.0)
    row_scale = jnp.exp(jax.random.uniform(row_key, (SEQS, LEN, 1), jnp.float32, math.log(0.3), math.log(3.0)))
    column_scale = jnp.exp(jax.random.uniform(column_key, (1, 1, D), jnp.float32, math.log(0.5), math.log(5.0)))
    return base_rows * row_scale * column_scale


def draw_w_qkv(key, part):
    value_key = jax.random.fold_in(key, 0)
    matrix = jnp.clip(jax.random.normal(value_key, (LAYERS, D, 3 * D), jnp.float32), -4.0, 4.0) * D ** (-0.5)
    return matrix.astype(jnp.bfloat16)


def block_levels(rng, dims, cuts, least, high):
    def one(position, shards_of):
        draws = jax.random.uniform(jax.random.fold_in(jax.random.fold_in(rng, 6), position), (shards_of,), jnp.float32, least / len(cuts), high / len(cuts))
        return jnp.repeat(jnp.exp(draws), dims[position] // shards_of).reshape((-1,) + (1,) * (len(dims) - position - 1))

    loudness = one(*cuts[0])
    for cut in cuts[1:]:
        loudness = loudness * one(*cut)
    return loudness


def normal_values(stream_key, extent, width, reach, pieces=(), held_as=jnp.bfloat16):
    gain = block_levels(stream_key, extent, pieces, -0.22, 0.18) if pieces else 1.0
    drawn = jax.random.normal(stream_key, extent, jnp.float32) * width * gain
    return jnp.minimum(jnp.maximum(drawn, -reach), reach).astype(held_as)


def setup_inputs(seed: int = 0) -> dict:
    splits = jax.random.split(jax.random.key(seed), 14)
    return {
        "latents": draw_latents(jax.random.fold_in(splits[13], 71), 0),
        "condition": normal_values(splits[1], (SEQS, D), 1.0, 5.0, ((0, 16),), jnp.float32),
        "cotangent": normal_values(splits[2], (SEQS, LEN, D), 1.0, 5.0, ((0, 16),), jnp.float32),
        "w_ada": normal_values(splits[3], (LAYERS, D, MOD), D ** -0.5, 0.3125, ((0, 2), (1, 4))),
        "b_ada": normal_values(splits[4], (LAYERS, MOD), 0.5, 3.0, ((0, 2), (1, 4))),
        "w_qkv": draw_w_qkv(jax.random.fold_in(splits[13], 71), 0),
        "b_qv": normal_values(splits[6], (LAYERS, 2 * D), 0.5, 3.0, ((0, 2), (1, 4))),
        "w_proj": normal_values(splits[7], (LAYERS, D, D), (D // 16) ** -0.5, 1.25, ((0, 2), (1, 4))),
        "b_proj": normal_values(splits[8], (LAYERS, D), 0.5, 3.0, ((0, 2), (1, 4))),
        "w_fc1": normal_values(splits[9], (LAYERS, D, FF), D ** -0.5, 0.3125, ((0, 2), (1, 4))),
        "b_fc1": normal_values(splits[10], (LAYERS, FF), 0.5, 3.0, ((0, 2), (1, 4))),
        "w_fc2": normal_values(splits[11], (LAYERS, FF, D), FF ** -0.5, 0.15625, ((0, 2), (1, 4))),
        "b_fc2": normal_values(splits[12], (LAYERS, D), 0.5, 3.0, ((0, 2), (1, 4))),
    }


EPSILON = 1e-06
GELU_C = 0.7978845608028654
CUBIC = 0.044715

def split_heads(matrix):
    return matrix.reshape(matrix.shape[0], HEADS, HEAD_DIM)

def norm_rows(stream):
    centred = stream - lax.optimization_barrier(jnp.mean(stream, axis=-1, keepdims=True))
    rstd_rows = lax.rsqrt(lax.optimization_barrier(jnp.mean(centred * centred, axis=-1, keepdims=True)) + EPSILON)
    return (centred * rstd_rows, rstd_rows)

def norm_back(grad_normed, normed, rstd_rows):
    return rstd_rows * (grad_normed - lax.optimization_barrier(jnp.mean(grad_normed, axis=-1, keepdims=True)) - normed * lax.optimization_barrier(jnp.mean(grad_normed * normed, axis=-1, keepdims=True)))

def gelu_value(hidden):
    tanh_part = jnp.tanh(GELU_C * (hidden + CUBIC * hidden * hidden * hidden))
    return 0.5 * hidden * (1.0 + tanh_part)

def gelu_slope(hidden):
    tanh_part = jnp.tanh(GELU_C * (hidden + CUBIC * hidden * hidden * hidden))
    return 0.5 * (1.0 + tanh_part) + 0.5 * hidden * (1.0 - tanh_part * tanh_part) * GELU_C * (1.0 + 3.0 * CUBIC * hidden * hidden)

def head_scores(queries, key_proj):
    return jnp.einsum('qhd,khd->hqk', split_heads(queries).astype(jnp.float32), split_heads(key_proj).astype(jnp.float32)) * HEAD_DIM ** (-0.5)

def layer_forward(stream, cond_row, params):
    w_ada, b_ada, w_qkv, b_qv, w_proj, b_proj, w_fc1, b_fc1, w_fc2, b_fc2 = params
    model_width = stream.shape[1]
    row_count = stream.shape[0]
    act = jax.nn.silu(cond_row).astype(jnp.bfloat16)
    modulation = jnp.dot(act, w_ada, preferred_element_type=jnp.float32) + b_ada.astype(jnp.float32)
    shift_one, scale_one, gate_one, shift_two, scale_two, gate_two = jnp.split(modulation, 6, axis=1)
    normed_one, rstd_one = norm_rows(stream)
    input_one = (normed_one * (1.0 + scale_one) + shift_one).astype(jnp.bfloat16)
    triple = jnp.dot(input_one, w_qkv, preferred_element_type=jnp.float32)
    bias_qv = b_qv.astype(jnp.float32)
    queries = (triple[:, :model_width] + bias_qv[:model_width]).astype(jnp.bfloat16)
    key_proj = triple[:, model_width:2 * model_width].astype(jnp.bfloat16)
    values = (triple[:, 2 * model_width:] + bias_qv[model_width:]).astype(jnp.bfloat16)
    scores = head_scores(queries, key_proj)
    row_max = lax.optimization_barrier(jnp.max(scores, axis=-1, keepdims=True))
    logsum = row_max + jnp.log(lax.optimization_barrier(jnp.sum(jnp.exp(scores - row_max), axis=-1, keepdims=True)))
    attention_probs = jnp.exp(scores - logsum).astype(jnp.bfloat16)
    heads_out = jnp.einsum('hqk,khd->qhd', attention_probs.astype(jnp.float32), split_heads(values).astype(jnp.float32))
    heads_out = heads_out.reshape(row_count, model_width).astype(jnp.bfloat16)
    attended = jnp.dot(heads_out, w_proj, preferred_element_type=jnp.float32) + b_proj.astype(jnp.float32)
    middle = stream + gate_one * attended
    normed_two, rstd_two = norm_rows(middle)
    input_two = (normed_two * (1.0 + scale_two) + shift_two).astype(jnp.bfloat16)
    hidden = jnp.dot(input_two, w_fc1, preferred_element_type=jnp.float32) + b_fc1.astype(jnp.float32)
    activated = gelu_value(hidden).astype(jnp.bfloat16)
    projected = jnp.dot(activated, w_fc2, preferred_element_type=jnp.float32) + b_fc2.astype(jnp.float32)
    output = middle + gate_two * projected
    saved = (act, modulation, normed_one, rstd_one, input_one, queries, key_proj, values, logsum, heads_out, attended, normed_two, rstd_two, input_two, hidden, activated, projected)
    return (output, saved)

def layer_backward(grad_out, saved, cond_row, params):
    w_ada, b_ada, w_qkv, b_qv, w_proj, b_proj, w_fc1, b_fc1, w_fc2, b_fc2 = params
    act, modulation, normed_one, rstd_one, input_one, queries, key_proj, values, logsum, heads_out, attended, normed_two, rstd_two, input_two, hidden, activated, projected = saved
    row_count = grad_out.shape[0]
    shift_one, scale_one, gate_one, shift_two, scale_two, gate_two = jnp.split(modulation, 6, axis=1)
    grad_gate_two = lax.optimization_barrier(jnp.sum(grad_out * projected, axis=0, keepdims=True))
    grad_proj = grad_out * gate_two
    grad_proj_b = grad_proj.astype(jnp.bfloat16)
    grad_w_fc2 = jnp.dot(activated.T, grad_proj_b, preferred_element_type=jnp.float32)
    grad_b_fc2 = lax.optimization_barrier(jnp.sum(grad_proj, axis=0))
    grad_hidden = jnp.dot(grad_proj_b, w_fc2.T, preferred_element_type=jnp.float32) * gelu_slope(hidden)
    grad_hidden_b = grad_hidden.astype(jnp.bfloat16)
    grad_w_fc1 = jnp.dot(input_two.T, grad_hidden_b, preferred_element_type=jnp.float32)
    grad_b_fc1 = lax.optimization_barrier(jnp.sum(grad_hidden, axis=0))
    grad_in_two = jnp.dot(grad_hidden_b, w_fc1.T, preferred_element_type=jnp.float32)
    grad_scale_two = lax.optimization_barrier(jnp.sum(grad_in_two * normed_two, axis=0, keepdims=True))
    grad_shift_two = lax.optimization_barrier(jnp.sum(grad_in_two, axis=0, keepdims=True))
    grad_middle = grad_out + norm_back(grad_in_two * (1.0 + scale_two), normed_two, rstd_two)
    grad_gate_one = lax.optimization_barrier(jnp.sum(grad_middle * attended, axis=0, keepdims=True))
    grad_att = grad_middle * gate_one
    grad_att_b = grad_att.astype(jnp.bfloat16)
    grad_w_proj = jnp.dot(heads_out.T, grad_att_b, preferred_element_type=jnp.float32)
    grad_b_proj = lax.optimization_barrier(jnp.sum(grad_att, axis=0))
    grad_heads = jnp.dot(grad_att_b, w_proj.T, preferred_element_type=jnp.float32).astype(jnp.bfloat16)
    scores = head_scores(queries, key_proj)
    attention_probs = jnp.exp(scores - logsum)
    probs_b = attention_probs.astype(jnp.bfloat16)
    grad_heads_h = split_heads(grad_heads).astype(jnp.float32)
    grad_values = jnp.einsum('hqk,qhd->khd', probs_b.astype(jnp.float32), grad_heads_h)
    grad_probs = jnp.einsum('qhd,khd->hqk', grad_heads_h, split_heads(values).astype(jnp.float32))
    row_total = lax.optimization_barrier(jnp.sum(attention_probs * grad_probs, axis=-1, keepdims=True))
    grad_scores = (attention_probs * (grad_probs - row_total) * HEAD_DIM ** (-0.5)).astype(jnp.bfloat16)
    grad_queries = jnp.einsum('hqk,khd->qhd', grad_scores.astype(jnp.float32), split_heads(key_proj).astype(jnp.float32))
    grad_keys = jnp.einsum('hqk,qhd->khd', grad_scores.astype(jnp.float32), split_heads(queries).astype(jnp.float32))
    grad_queries = grad_queries.reshape(row_count, -1)
    grad_keys = grad_keys.reshape(row_count, -1)
    grad_values = grad_values.reshape(row_count, -1)
    grad_triple_b = jnp.concatenate([grad_queries, grad_keys, grad_values], axis=1).astype(jnp.bfloat16)
    grad_w_qkv = jnp.dot(input_one.T, grad_triple_b, preferred_element_type=jnp.float32)
    grad_b_qv = jnp.concatenate([lax.optimization_barrier(jnp.sum(grad_queries, axis=0)), lax.optimization_barrier(jnp.sum(grad_values, axis=0))])
    grad_in_one = jnp.dot(grad_triple_b, w_qkv.T, preferred_element_type=jnp.float32)
    grad_scale_one = lax.optimization_barrier(jnp.sum(grad_in_one * normed_one, axis=0, keepdims=True))
    grad_shift_one = lax.optimization_barrier(jnp.sum(grad_in_one, axis=0, keepdims=True))
    grad_input = grad_middle + norm_back(grad_in_one * (1.0 + scale_one), normed_one, rstd_one)
    grad_mod = jnp.concatenate([grad_shift_one, grad_scale_one, grad_gate_one, grad_shift_two, grad_scale_two, grad_gate_two], axis=1)
    grad_mod_b = grad_mod.astype(jnp.bfloat16)
    grad_w_ada = jnp.dot(act.T, grad_mod_b, preferred_element_type=jnp.float32)
    grad_b_ada = grad_mod[0]
    grad_silu = jnp.dot(grad_mod_b, w_ada.T, preferred_element_type=jnp.float32)
    sigmoid_cond = jax.nn.sigmoid(cond_row)
    grad_cond = grad_silu * sigmoid_cond * (1.0 + cond_row * (1.0 - sigmoid_cond))
    grads = (grad_w_ada, grad_b_ada, grad_w_qkv, grad_b_qv, grad_w_proj, grad_b_proj, grad_w_fc1, grad_b_fc1, grad_w_fc2, grad_b_fc2)
    return (grad_input, grad_cond, grads)

def reference(latents, condition, cotangent, w_ada, b_ada, w_qkv, b_qv, w_proj, b_proj, w_fc1, b_fc1, w_fc2, b_fc2):
    stacked_weights = (w_ada, b_ada, w_qkv, b_qv, w_proj, b_proj, w_fc1, b_fc1, w_fc2, b_fc2)
    layer_count = w_ada.shape[0]
    streams = [latents]
    for layer_index in range(layer_count):
        params = tuple((array[layer_index] for array in stacked_weights))

        def run_one(sample, params=params):
            return layer_forward(sample[0], sample[1][None, :], params)[0]
        streams.append(lax.map(run_one, (streams[-1], condition)))
    grad_stream = cotangent
    input_list = [None] * layer_count
    grad_list = [None] * layer_count
    cond_grad = jnp.zeros(condition.shape, jnp.float32)
    for layer_index in reversed(range(layer_count)):
        params = tuple((array[layer_index] for array in stacked_weights))

        def run_back(totals, sample, params=params):
            stream, cond_row, grad_out = sample
            cond_row = cond_row[None, :]
            output, saved = layer_forward(stream, cond_row, params)
            grad_input, grad_cond, grads = layer_backward(grad_out, saved, cond_row, params)
            return (tuple((running + term for running, term in zip(totals, grads))), (grad_input, grad_cond[0]))
        initial = tuple((jnp.zeros(array.shape, jnp.float32) for array in params))
        totals, (grad_stream, cond_part) = lax.scan(run_back, initial, (streams[layer_index], condition, grad_stream))
        input_list[layer_index] = grad_stream
        grad_list[layer_index] = totals
        cond_grad = cond_grad + cond_part
    return (jnp.stack(streams[1:]), jnp.stack(input_list), cond_grad, jnp.stack([grads[0] for grads in grad_list]), jnp.stack([grads[1] for grads in grad_list]), jnp.stack([grads[2] for grads in grad_list]), jnp.stack([grads[3] for grads in grad_list]), jnp.stack([grads[4] for grads in grad_list]), jnp.stack([grads[5] for grads in grad_list]), jnp.stack([grads[6] for grads in grad_list]), jnp.stack([grads[7] for grads in grad_list]), jnp.stack([grads[8] for grads in grad_list]), jnp.stack([grads[9] for grads in grad_list]))
```

```python
import jax
import jax.numpy as jnp
from jax import lax
from jax.experimental import pallas as pl
from jax.experimental.pallas import tpu as pltpu
from jax.sharding import PartitionSpec as P


HEADS = 6
HEAD_DIM = 64
EPSILON = 1e-06
GELU_C = 0.7978845608028654
CUBIC = 0.044715
F32 = jnp.float32
BF16 = jnp.bfloat16
VMEM_LIMIT = 48 * 1024 * 1024
AUX_ROWS = 32


def xor_permute(array, axis, mask):
    return lax.ppermute(array, axis, [(i, i ^ mask) for i in range(lax.axis_size(axis))])


def pick(array, index):
    return lax.dynamic_index_in_dim(array, index, 0, keepdims=False)


def added(*parts):
    total = parts[0].astype(F32)
    for part in parts[1:]:
        total = total + part.astype(F32)
    return total


def nn(left, right):
    return lax.dot_general(left, right, (((1,), (0,)), ((), ())), preferred_element_type=F32)


def nt(left, right):
    return lax.dot_general(left, right, (((1,), (1,)), ((), ())), preferred_element_type=F32)


def tn(left, right):
    return lax.dot_general(left, right, (((0,), (0,)), ((), ())), preferred_element_type=F32)


def row_norm(stream):
    centred = stream - jnp.mean(stream, axis=-1, keepdims=True)
    rstd = lax.rsqrt(jnp.mean(centred * centred, axis=-1, keepdims=True) + EPSILON)
    return centred * rstd, rstd


def row_norm_back(grad, normed, rstd):
    return rstd * (
        grad
        - jnp.mean(grad, axis=-1, keepdims=True)
        - normed * jnp.mean(grad * normed, axis=-1, keepdims=True)
    )


def column_sum(value):
    return jnp.sum(value, axis=0, keepdims=True)


SMEM_SPEC = pl.BlockSpec(memory_space=pltpu.SMEM)
ANY_SPEC = pl.BlockSpec(memory_space=pl.ANY)


def whole(shape):
    return pl.BlockSpec(shape, lambda i: (0,) * len(shape))


def per_latent(shape):
    return pl.BlockSpec((None,) + shape, lambda i: (i,) + (0,) * len(shape))


def shaped(shape, dtype):
    return jax.ShapeDtypeStruct(shape, dtype)


PARAMS = pltpu.CompilerParams(vmem_limit_bytes=VMEM_LIMIT)


def pack_kernel(where_ref, qkv_ref, proj_ref, fc1_ref, fc2_ref, act_ref, out_b_ref, out_a_ref):
    quarter = where_ref[2]
    rows, width = proj_ref.shape
    out_b_ref[rows:, :] = act_ref[...]
    half = fc2_ref.shape[0] // 2
    for j in range(4):

        @pl.when(quarter == j)
        def _(j=j):
            if j < 3:
                out_b_ref[:rows, :] = qkv_ref[:, j * width : (j + 1) * width]
            else:
                out_b_ref[:rows, :] = proj_ref[...]
            if j < 2:
                out_a_ref[:rows, :] = fc1_ref[:, 2 * j * width : (2 * j + 1) * width]
                out_a_ref[rows:, :] = fc1_ref[:, (2 * j + 1) * width : (2 * j + 2) * width]
            else:
                out_a_ref[...] = fc2_ref[(j - 2) * half : (j - 1) * half, :]


def pack(where, w_qkv, w_proj, w_fc1, w_fc2, act_rows):
    rows, width = w_proj.shape
    vmem = pl.BlockSpec(memory_space=pltpu.VMEM)
    return pl.pallas_call(
        pack_kernel,
        in_specs=[SMEM_SPEC] + [vmem] * 5,
        out_specs=[vmem, vmem],
        out_shape=[shaped((rows + 16, width), BF16), shaped((2 * rows, width), BF16)],
        compiler_params=PARAMS,
        name="pack",
    )(where, w_qkv, w_proj, w_fc1, w_fc2, act_rows)


def assemble_b_kernel(where_ref, own_ref, other_ref, qkv_ref, proj_ref, sems):
    place, quarter = where_ref[1], where_ref[2]
    width = proj_ref.shape[1]
    shards = own_ref.shape[1]
    rows = proj_ref.shape[0] // shards
    for start in (True, False):
        for core, ref in ((0, own_ref), (1, other_ref)):
            for side in range(2):
                target = quarter ^ (core + 2 * side)
                column = pl.multiple_of(jnp.minimum(target, 2) * width, 128)
                for k in range(shards):
                    row = pl.multiple_of((place ^ k) * rows, 16)
                    source = ref.at[side, k, pl.ds(0, rows), :]
                    sem = sems.at[core, side, k]
                    into_proj = proj_ref.at[pl.ds(row, rows), :]
                    if not start:
                        pltpu.make_async_copy(source, into_proj, sem).wait()
                        continue
                    into_qkv = qkv_ref.at[pl.ds(row, rows), pl.ds(column, width)]

                    @pl.when(target < 3)
                    def _(source=source, into_qkv=into_qkv, sem=sem):
                        pltpu.make_async_copy(source, into_qkv, sem).start()

                    @pl.when(target == 3)
                    def _(source=source, into_proj=into_proj, sem=sem):
                        pltpu.make_async_copy(source, into_proj, sem).start()


def assemble_b(where, own, other):
    _, shards, padded, width = own.shape
    rows = padded - 16
    return pl.pallas_call(
        assemble_b_kernel,
        in_specs=[SMEM_SPEC, ANY_SPEC, ANY_SPEC],
        out_specs=[ANY_SPEC, ANY_SPEC],
        out_shape=[
            shaped((shards * rows, 3 * width), BF16),
            shaped((shards * rows, width), BF16),
        ],
        scratch_shapes=[pltpu.SemaphoreType.DMA((2, 2, shards))],
        compiler_params=PARAMS,
        name="assemble_b",
    )(where, own, other)


def assemble_a_kernel(where_ref, own_ref, other_ref, fc1_ref, fc2_ref, sems):
    place, quarter = where_ref[1], where_ref[2]
    width = fc2_ref.shape[1]
    shards = own_ref.shape[1]
    rows = fc1_ref.shape[0] // shards
    for start in (True, False):
        for core, ref in ((0, own_ref), (1, other_ref)):
            for side in range(2):
                target = quarter ^ (core + 2 * side)
                low = jnp.minimum(target, 1)
                high = jnp.maximum(target, 2) - 2
                for k in range(shards):
                    row = pl.multiple_of((place ^ k) * rows, 16)
                    deep = (place ^ k) * (4 * rows) + high * (2 * rows)
                    for part in range(2):
                        column = pl.multiple_of((2 * low + part) * width, 128)
                        source = ref.at[side, k, pl.ds(part * rows, rows), :]
                        sem = sems.at[core, side, k, part]
                        below = pl.multiple_of(deep + part * rows, 16)
                        into_fc2 = fc2_ref.at[pl.ds(below, rows), :]
                        if not start:
                            pltpu.make_async_copy(source, into_fc2, sem).wait()
                            continue
                        into_fc1 = fc1_ref.at[pl.ds(row, rows), pl.ds(column, width)]

                        @pl.when(target < 2)
                        def _(source=source, into_fc1=into_fc1, sem=sem):
                            pltpu.make_async_copy(source, into_fc1, sem).start()

                        @pl.when(target >= 2)
                        def _(source=source, into_fc2=into_fc2, sem=sem):
                            pltpu.make_async_copy(source, into_fc2, sem).start()


def assemble_a(where, own, other):
    _, shards, padded, width = own.shape
    rows = padded // 2
    return pl.pallas_call(
        assemble_a_kernel,
        in_specs=[SMEM_SPEC, ANY_SPEC, ANY_SPEC],
        out_specs=[ANY_SPEC, ANY_SPEC],
        out_shape=[
            shaped((shards * rows, 4 * width), BF16),
            shaped((shards * rows * 4, width), BF16),
        ],
        scratch_shapes=[pltpu.SemaphoreType.DMA((2, 2, shards, 2))],
        compiler_params=PARAMS,
        name="assemble_a",
    )(where, own, other)


def spread(piece):
    shards = [piece] + [
        xor_permute(piece, "fsdp", k) for k in range(1, lax.axis_size("fsdp"))
    ]
    return jnp.stack(shards)


def gathered(stacked):
    both = jnp.stack([stacked, xor_permute(stacked, "replica", 2)])
    return both, xor_permute(both, "replica", 1)


def own_columns(place, count, width):
    row = lax.broadcasted_iota(jnp.int32, (count, width), 0)
    column = lax.broadcasted_iota(jnp.int32, (count, width), 1)
    return column == row + place * count


def modulate_kernel(where_ref, stack_ref, w_ada_ref, b_ada_ref, bias_ref, out_ref):
    place = where_ref[1]
    rows, _ = w_ada_ref.shape
    shards, padded, width = stack_ref.shape
    latents = 2
    chosen = own_columns(place, rows, width).astype(F32).astype(BF16)
    for k in range(shards):
        act = stack_ref[k, padded - 16 :, :]
        mine = nt(act, chosen).astype(BF16)
        part = nn(mine, w_ada_ref[...])
        for latent in range(latents):
            for j in range(6):
                columns = slice(j * width, (j + 1) * width)
                out_ref[k, latent * 8 + j : latent * 8 + j + 1, :] = (
                    part[latent : latent + 1, columns] + b_ada_ref[:, columns]
                )
        out_ref[k, 2 * 8 : 3 * 8, :] = bias_ref[...]


def modulate(where, stack_b, w_ada, b_ada_row, bias_rows):
    shards = stack_b.shape[0]
    width = stack_b.shape[2]
    vmem = pl.BlockSpec(memory_space=pltpu.VMEM)
    return pl.pallas_call(
        modulate_kernel,
        in_specs=[SMEM_SPEC] + [vmem] * 4,
        out_specs=vmem,
        out_shape=shaped((shards, 24, width), F32),
        compiler_params=PARAMS,
        name="modulate",
    )(where, stack_b, w_ada, b_ada_row, bias_rows)


def chosen_stream(where_ref, own_ref, received_ref, section):
    if received_ref is None:
        return own_ref[...]
    return jnp.where(where_ref[0] == section, own_ref[...], received_ref[...].astype(F32))


def attention_forward(has_received, save):

    def kernel(where_ref, *refs):
        refs = list(refs)
        own_ref = refs.pop(0)
        received_ref = refs.pop(0) if has_received else None
        mod_ref, bias_ref, w_qkv_ref, w_proj_ref, middle_ref = refs[:5]
        width = w_proj_ref.shape[1]
        stream = chosen_stream(where_ref, own_ref, received_ref, 0)
        normed, _ = row_norm(stream)
        enter = (normed * (1.0 + mod_ref[1:2, :]) + mod_ref[0:1, :]).astype(BF16)
        triple = nn(enter, w_qkv_ref[...])
        queries = (triple[:, :width] + bias_ref[0:1, :]).astype(BF16)
        keys = triple[:, width : 2 * width].astype(BF16)
        values = (triple[:, 2 * width :] + bias_ref[1:2, :]).astype(BF16)
        queries_t = (queries * BF16(HEAD_DIM ** (-0.5))).T
        keys_t = keys.T
        values_t = values.T
        outputs = []
        for head in range(HEADS):
            span = slice(head * HEAD_DIM, (head + 1) * HEAD_DIM)
            scores = tn(keys_t[span], queries_t[span])
            powers = jnp.exp(scores - jnp.max(scores, axis=0, keepdims=True))
            probs = (powers * (1.0 / column_sum(powers))).astype(BF16)
            if save:
                refs[7][head] = probs
            outputs.append(nn(values_t[span], probs).astype(BF16))
        heads_out = jnp.concatenate(outputs, axis=0).T
        attended = nn(heads_out, w_proj_ref[...]) + bias_ref[2:3, :]
        middle_ref[...] = stream + mod_ref[2:3, :] * attended
        if save:
            refs[5][...] = enter
            refs[6][0] = queries_t
            refs[6][1] = keys_t
            refs[6][2] = values_t
            refs[8][...] = heads_out
            refs[9][...] = attended.astype(BF16)

    return kernel


def run_attention_forward(where, own, received, mod, bias, w_qkv, w_proj, save):
    count, length, width = own.shape
    stream = per_latent((length, width))
    operands = [own] + ([received] if received is not None else [])
    outs = [((length, width), F32)]
    if save:
        outs += [
            ((length, width), BF16),
            ((3, width, length), BF16),
            ((HEADS, length, length), BF16),
            ((length, width), BF16),
            ((length, width), BF16),
        ]
    return pl.pallas_call(
        attention_forward(received is not None, save),
        grid=(count,),
        in_specs=[SMEM_SPEC]
        + [stream] * len(operands)
        + [per_latent(mod.shape[1:]), whole(bias.shape), whole(w_qkv.shape), whole(w_proj.shape)],
        out_specs=[per_latent(shape) for shape, _ in outs],
        out_shape=[shaped((count,) + shape, dtype) for shape, dtype in outs],
        compiler_params=PARAMS,
        name="attention_forward",
    )(where, *operands, mod, bias, w_qkv, w_proj)


def feed_forward(save):

    def kernel(middle_ref, mod_ref, bias_ref, w_fc1_ref, w_fc2_ref, out_ref, *refs):
        width = w_fc2_ref.shape[1]
        middle = middle_ref[...]
        normed, _ = row_norm(middle)
        enter = (normed * (1.0 + mod_ref[4:5, :]) + mod_ref[3:4, :]).astype(BF16)
        projected = bias_ref[7:8, :]
        for j in range(4):
            span = slice(j * width, (j + 1) * width)
            hidden = nn(enter, w_fc1_ref[:, span]) + bias_ref[3 + j : 4 + j, :]
            square = hidden * hidden
            tanh_part = jnp.tanh((GELU_C * hidden) * (1.0 + CUBIC * square))
            half_sum = 0.5 * (1.0 + tanh_part)
            active = (hidden * half_sum).astype(BF16)
            projected = projected + nn(active, w_fc2_ref[span, :])
            if save:
                slope = half_sum + (0.5 * GELU_C) * hidden * (1.0 - tanh_part * tanh_part) * (
                    1.0 + (3.0 * CUBIC) * square
                )
                refs[1][:, span] = active
                refs[2][:, span] = slope.astype(BF16)
        result = middle + mod_ref[5:6, :] * projected
        out_ref[...] = result.astype(out_ref.dtype)
        if save:
            refs[0][...] = enter
            refs[3][...] = projected.astype(BF16)

    return kernel


def run_feed_forward(middle, mod, bias, w_fc1, w_fc2, save):
    count, length, width = middle.shape
    hidden = w_fc1.shape[1]
    outs = [((length, width), F32 if save else BF16)]
    if save:
        outs += [
            ((length, width), BF16),
            ((length, hidden), BF16),
            ((length, hidden), BF16),
            ((length, width), BF16),
        ]
    return pl.pallas_call(
        feed_forward(save),
        grid=(count,),
        in_specs=[
            per_latent((length, width)),
            per_latent(mod.shape[1:]),
            whole(bias.shape),
            whole(w_fc1.shape),
            whole(w_fc2.shape),
        ],
        out_specs=[per_latent(shape) for shape, _ in outs],
        out_shape=[shaped((count,) + shape, dtype) for shape, dtype in outs],
        compiler_params=PARAMS,
        name="feed_forward",
    )(middle, mod, bias, w_fc1, w_fc2)


def feed_backward(has_received, last, save):

    def kernel(where_ref, *refs):
        refs = list(refs)
        own_ref = refs.pop(0)
        received_ref = refs.pop(0) if has_received else None
        middle_ref, mod_ref, w_fc1_ref, w_fc2_ref, slope_ref, projected_ref = refs[:6]
        out_ref = refs[6]
        width = w_fc2_ref.shape[1]
        grad_out = chosen_stream(where_ref, own_ref, received_ref, last)
        grad_proj = grad_out * mod_ref[5:6, :]
        grad_proj_b = grad_proj.astype(BF16)
        grad_in = 0.0
        for j in range(4):
            span = slice(j * width, (j + 1) * width)
            grad_hidden = nt(grad_proj_b, w_fc2_ref[span, :]) * slope_ref[:, span].astype(F32)
            grad_hidden_b = grad_hidden.astype(BF16)
            grad_in = grad_in + nt(grad_hidden_b, w_fc1_ref[:, span])
            if save:
                refs[8][:, span] = grad_hidden_b
                refs[9][4 + j : 5 + j, :] = column_sum(grad_hidden)
        normed, rstd = row_norm(middle_ref[...])
        out_ref[...] = grad_out + row_norm_back(grad_in * (1.0 + mod_ref[4:5, :]), normed, rstd)
        if save:
            refs[7][...] = grad_proj_b
            refs[9][0:1, :] = column_sum(grad_in)
            refs[9][1:2, :] = column_sum(grad_in * normed)
            refs[9][2:3, :] = column_sum(grad_out * projected_ref[...].astype(F32))
            refs[9][3:4, :] = column_sum(grad_proj)

    return kernel


def run_feed_backward(where, own, received, middle, mod, w_fc1, w_fc2, slope, projected, last, save):
    count, length, width = own.shape
    hidden = w_fc1.shape[1]
    stream = per_latent((length, width))
    operands = [own] + ([received] if received is not None else [])
    outs = [((length, width), F32)]
    if save:
        outs += [((length, width), BF16), ((length, hidden), BF16), ((8, width), F32)]
    return pl.pallas_call(
        feed_backward(received is not None, last, save),
        grid=(count,),
        in_specs=[SMEM_SPEC]
        + [stream] * len(operands)
        + [
            stream,
            per_latent(mod.shape[1:]),
            whole(w_fc1.shape),
            whole(w_fc2.shape),
            per_latent((length, hidden)),
            stream,
        ],
        out_specs=[per_latent(shape) for shape, _ in outs],
        out_shape=[shaped((count,) + shape, dtype) for shape, dtype in outs],
        compiler_params=PARAMS,
        name="feed_backward",
    )(where, *operands, middle, mod, w_fc1, w_fc2, slope, projected)


def attention_backward(has_received, save):

    def kernel(where_ref, *refs):
        refs = list(refs)
        own_ref = refs.pop(0)
        received_ref = refs.pop(0) if has_received else None
        grad_ref, mod_ref, w_qkv_ref, w_proj_ref, triple_ref, probs_ref, attended_ref = refs[:7]
        out_ref = refs[7]
        width = w_proj_ref.shape[1]
        grad_middle = grad_ref[...]
        grad_att = grad_middle * mod_ref[2:3, :]
        grad_att_b = grad_att.astype(BF16)
        grad_heads = nt(w_proj_ref[...], grad_att_b).astype(BF16)
        parts = [[], [], []]
        for head in range(HEADS):
            span = slice(head * HEAD_DIM, (head + 1) * HEAD_DIM)
            grad_head = grad_heads[span]
            probs_b = probs_ref[head]
            probs = probs_b.astype(F32)
            grad_probs = tn(triple_ref[2, span, :], grad_head)
            total = column_sum(probs * grad_probs)
            grad_scores = (probs * (grad_probs - total)).astype(BF16)
            scale = HEAD_DIM ** (-0.5)
            parts[0].append((nn(triple_ref[1, span, :], grad_scores) * scale).astype(BF16))
            parts[1].append(nt(triple_ref[0, span, :], grad_scores).astype(BF16))
            parts[2].append(nt(grad_head, probs_b).astype(BF16))
        grad_triple = jnp.concatenate(
            [jnp.concatenate(part, axis=0).T for part in parts], axis=1
        )
        grad_in = nt(grad_triple, w_qkv_ref[...])
        normed, rstd = row_norm(chosen_stream(where_ref, own_ref, received_ref, 0))
        result = grad_middle + row_norm_back(grad_in * (1.0 + mod_ref[1:2, :]), normed, rstd)
        out_ref[...] = result.astype(out_ref.dtype)
        if save:
            refs[8][...] = grad_att_b
            refs[9][...] = grad_triple
            refs[10][0:1, :] = column_sum(grad_in)
            refs[10][1:2, :] = column_sum(grad_in * normed)
            refs[10][2:3, :] = column_sum(grad_middle * attended_ref[...].astype(F32))
            refs[10][3:4, :] = column_sum(grad_att)
            refs[10][4:5, :] = column_sum(grad_triple[:, :width].astype(F32))
            refs[10][5:6, :] = column_sum(grad_triple[:, 2 * width :].astype(F32))
            refs[10][6:8, :] = jnp.zeros((2, width), F32)

    return kernel


def run_attention_backward(
    where, own, received, grad, mod, w_qkv, w_proj, triple, probs, attended, save
):
    count, length, width = own.shape
    stream = per_latent((length, width))
    operands = [own] + ([received] if received is not None else [])
    outs = [((length, width), F32 if save else BF16)]
    if save:
        outs += [((length, width), BF16), ((length, 3 * width), BF16), ((8, width), F32)]
    return pl.pallas_call(
        attention_backward(received is not None, save),
        grid=(count,),
        in_specs=[SMEM_SPEC]
        + [stream] * len(operands)
        + [
            stream,
            per_latent(mod.shape[1:]),
            whole(w_qkv.shape),
            whole(w_proj.shape),
            per_latent(triple.shape[1:]),
            per_latent(probs.shape[1:]),
            stream,
        ],
        out_specs=[per_latent(shape) for shape, _ in outs],
        out_shape=[shaped((count,) + shape, dtype) for shape, dtype in outs],
        compiler_params=PARAMS,
        name="attention_backward",
    )(where, *operands, grad, mod, w_qkv, w_proj, triple, probs, attended)


def split_out(where_ref, both_ref, send_ref, keep_ref):
    core = where_ref[3]
    keep_ref[...] = both_ref[core]
    send_ref[...] = both_ref[1 - core]


def weights_a_kernel(
    where_ref, active_ref, grad_proj_ref, enter_ref, grad_hidden_ref, send_ref, keep_ref, both_ref
):
    _, _, shards, two_rows, width = both_ref.shape
    rows = two_rows // 2
    for j in range(4):
        span = slice(j * width, (j + 1) * width)
        block = tn(enter_ref[...], grad_hidden_ref[:, span]).astype(BF16)
        quarter, part = j // 2, j % 2
        for k in range(shards):
            both_ref[quarter & 1, quarter >> 1, k, part * rows : (part + 1) * rows, :] = block[
                k * rows : (k + 1) * rows
            ]
    deep = 4 * rows
    step = 4 * width // 4
    for j in range(4):
        block = tn(active_ref[:, j * step : (j + 1) * step], grad_proj_ref[...]).astype(BF16)
        for first in range(0, step, 2 * rows):
            row = j * step + first
            quarter = 2 + (row % deep) // (2 * rows)
            both_ref[quarter & 1, quarter >> 1, row // deep] = block[first : first + 2 * rows]
    split_out(where_ref, both_ref, send_ref, keep_ref)


def weights_b_kernel(
    where_ref,
    enter_ref,
    grad_triple_ref,
    heads_ref,
    grad_att_ref,
    aux_one_ref,
    aux_two_ref,
    act_ref,
    send_ref,
    keep_ref,
    aux_ref,
    both_ref,
    rows_ref,
):
    _, _, shards, rows, width = both_ref.shape
    for quarter in range(4):
        if quarter < 3:
            span = slice(quarter * width, (quarter + 1) * width)
            block = tn(enter_ref[...], grad_triple_ref[:, span]).astype(BF16)
        else:
            block = tn(heads_ref[...], grad_att_ref[...]).astype(BF16)
        for k in range(shards):
            both_ref[quarter & 1, quarter >> 1, k] = block[k * rows : (k + 1) * rows]
    split_out(where_ref, both_ref, send_ref, keep_ref)
    rows_ref[...] = jnp.zeros(rows_ref.shape, F32)
    for latent in range(2):
        rows_ref[6 * latent : 6 * latent + 3, :] = aux_one_ref[latent, 0:3, :]
        rows_ref[6 * latent + 3 : 6 * latent + 6, :] = aux_two_ref[latent, 0:3, :]
    rows_ref[12:14, :] = aux_one_ref[0, 4:6, :] + aux_one_ref[1, 4:6, :]
    rows_ref[14:15, :] = aux_one_ref[0, 3:4, :] + aux_one_ref[1, 3:4, :]
    rows_ref[15:19, :] = aux_two_ref[0, 4:8, :] + aux_two_ref[1, 4:8, :]
    rows_ref[19:20, :] = aux_two_ref[0, 3:4, :] + aux_two_ref[1, 3:4, :]
    rows_ref[20:22, :] = act_ref[0:2, :].astype(F32)
    aux_ref[...] = rows_ref[...].astype(BF16)


def run_weights_a(where, shards, active, grad_proj, enter, grad_hidden):
    width = grad_proj.shape[1]
    rows = width // shards
    half = (2, shards, 2 * rows, width)
    vmem = pl.BlockSpec(memory_space=pltpu.VMEM)
    return pl.pallas_call(
        weights_a_kernel,
        in_specs=[SMEM_SPEC] + [vmem] * 4,
        out_specs=[vmem] * 2,
        out_shape=[shaped(half, BF16)] * 2,
        scratch_shapes=[pltpu.VMEM((2,) + half, BF16)],
        compiler_params=PARAMS,
        name="weights_a",
    )(where, active, grad_proj, enter, grad_hidden)


def run_weights_b(where, shards, enter, grad_triple, heads, grad_att, aux_one, aux_two, act_rows):
    width = grad_att.shape[1]
    rows = width // shards
    half = (2, shards, rows, width)
    vmem = pl.BlockSpec(memory_space=pltpu.VMEM)
    return pl.pallas_call(
        weights_b_kernel,
        in_specs=[SMEM_SPEC] + [vmem] * 7,
        out_specs=[vmem] * 3,
        out_shape=[shaped(half, BF16)] * 2 + [shaped((AUX_ROWS, width), BF16)],
        scratch_shapes=[pltpu.VMEM((2,) + half, BF16), pltpu.VMEM((AUX_ROWS, width), F32)],
        compiler_params=PARAMS,
        name="weights_b",
    )(where, enter, grad_triple, heads, grad_att, aux_one, aux_two, act_rows)


def reduced(send, keep, place, side):
    received = xor_permute(send, "replica", 1)
    outgoing = added(pick(keep, 1 - side), pick(received, 1 - side)).astype(BF16)
    arrived = xor_permute(outgoing, "replica", 2)
    staying = added(pick(keep, side), pick(received, side)).astype(BF16)
    total = added(pick(staying, place), pick(arrived, place))
    for k in range(1, lax.axis_size("fsdp")):
        there = place ^ k
        part = added(pick(staying, there), pick(arrived, there)).astype(BF16)
        total = total + xor_permute(part, "fsdp", k).astype(F32)
    bit = 4
    while bit < lax.axis_size("replica"):
        total = total + xor_permute(total.astype(BF16), "replica", bit).astype(F32)
        bit *= 2
    mine = total.astype(BF16)
    both = jnp.stack([mine, xor_permute(mine, "replica", 2)])
    return both, xor_permute(both, "replica", 1)


def finish_kernel(
    where_ref, own_a_ref, other_a_ref, own_b_ref, other_b_ref, qkv_ref, proj_ref, fc1_ref, fc2_ref
):
    quarter = where_ref[2]
    rows, width = proj_ref.shape
    for core in range(2):
        a_ref = (own_a_ref, other_a_ref)[core]
        b_ref = (own_b_ref, other_b_ref)[core]
        for side in range(2):
            target = quarter ^ (core + 2 * side)
            for j in range(4):

                @pl.when(target == j)
                def _(j=j, side=side, a_ref=a_ref, b_ref=b_ref):
                    part_b = b_ref[side].astype(F32)
                    part_a = a_ref[side].astype(F32)
                    if j < 3:
                        qkv_ref[:, j * width : (j + 1) * width] = part_b
                    else:
                        proj_ref[...] = part_b
                    if j < 2:
                        fc1_ref[:, 2 * j * width : (2 * j + 1) * width] = part_a[:rows]
                        fc1_ref[:, (2 * j + 1) * width : (2 * j + 2) * width] = part_a[rows:]
                    else:
                        fc2_ref[(j - 2) * 2 * rows : (j - 1) * 2 * rows, :] = part_a


def finish(where, own_a, other_a, own_b, other_b):
    rows, width = own_b.shape[1:]
    vmem = pl.BlockSpec(memory_space=pltpu.VMEM)
    return pl.pallas_call(
        finish_kernel,
        in_specs=[SMEM_SPEC] + [vmem] * 4,
        out_specs=[vmem] * 4,
        out_shape=[
            shaped((rows, 3 * width), F32),
            shaped((rows, width), F32),
            shaped((rows, 4 * width), F32),
            shaped((4 * rows, width), F32),
        ],
        compiler_params=PARAMS,
        name="finish",
    )(where, own_a, other_a, own_b, other_b)


def condition_kernel(where_ref, aux_ref, w_ada_ref, out_ref, rows_ref):
    place = where_ref[1]
    rows = w_ada_ref.shape[0]
    shards, _, width = aux_ref.shape
    for k in range(shards):
        part = aux_ref[k].astype(F32)
        for latent in range(2):
            for j in range(6):
                row = 6 * latent + j
                rows_ref[j, 2 * k + latent : 2 * k + latent + 1, :] = part[row : row + 1, :]
    total = 0.0
    for j in range(6):
        columns = slice(j * width, (j + 1) * width)
        total = total + nt(rows_ref[j].astype(BF16), w_ada_ref[:, columns])
    chosen = own_columns(place, rows, width).astype(F32)
    spread_out = lax.dot_general(
        total,
        chosen,
        (((1,), (0,)), ((), ())),
        preferred_element_type=F32,
        precision=lax.Precision.HIGHEST,
    )
    for k in range(shards):
        out_ref[k] = spread_out[2 * k : 2 * k + 2, :]


def run_condition(where, aux, w_ada):
    shards, _, width = aux.shape
    vmem = pl.BlockSpec(memory_space=pltpu.VMEM)
    return pl.pallas_call(
        condition_kernel,
        in_specs=[SMEM_SPEC, vmem, vmem],
        out_specs=vmem,
        out_shape=shaped((shards, 2, width), F32),
        scratch_shapes=[pltpu.VMEM((6, 2 * shards, width), F32)],
        compiler_params=PARAMS,
        name="condition_grad",
    )(where, aux, w_ada)


def ada_kernel(where_ref, aux_ref, grad_ref, sums_ref, rows_ref, act_ref):
    place = where_ref[1]
    rows = grad_ref.shape[0]
    devices, _, width = aux_ref.shape
    sums_ref[...] = jnp.zeros(sums_ref.shape, F32)

    def one(device, carry):
        part = aux_ref[device].astype(F32)
        for latent in range(2):
            at = 2 * device + latent
            for j in range(6):
                row = 6 * latent + j
                rows_ref[j, pl.ds(at, 1), :] = part[row : row + 1, :]
            act_ref[pl.ds(at, 1), :] = part[20 + latent : 21 + latent, :]
        sums_ref[0:8, :] = sums_ref[0:8, :] + part[12:20, :]
        return carry

    lax.fori_loop(0, devices, one, 0)
    chosen = own_columns(place, rows, width).astype(F32).astype(BF16)
    mine = nt(chosen, act_ref[...].astype(BF16)).astype(BF16)
    for j in range(6):
        columns = slice(j * width, (j + 1) * width)
        grad_ref[:, columns] = nn(mine, rows_ref[j].astype(BF16))
        sums_ref[8 + j : 9 + j, :] = column_sum(rows_ref[j])


def run_ada(where, aux, rows):
    devices, _, width = aux.shape
    vmem = pl.BlockSpec(memory_space=pltpu.VMEM)
    return pl.pallas_call(
        ada_kernel,
        in_specs=[SMEM_SPEC, vmem],
        out_specs=[vmem, vmem],
        out_shape=[shaped((rows, 6 * width), F32), shaped((16, width), F32)],
        scratch_shapes=[
            pltpu.VMEM((6, 2 * devices, width), F32),
            pltpu.VMEM((2 * devices, width), F32),
        ],
        compiler_params=PARAMS,
        name="ada_grad",
    )(where, aux)


def local(
    latents,
    condition,
    cotangent,
    w_ada,
    b_ada,
    w_qkv,
    b_qv,
    w_proj,
    b_proj,
    w_fc1,
    b_fc1,
    w_fc2,
    b_fc2,
):
    sections = lax.axis_size("section")
    shards = lax.axis_size("fsdp")
    section = lax.axis_index("section")
    place = lax.axis_index("fsdp")
    member = lax.axis_index("replica")
    quarter = member % 4
    core = member % 2
    side = quarter // 2
    where = jnp.stack([section, place, quarter, core]).astype(jnp.int32)
    count, length, width = latents.shape

    act_rows = jnp.pad(jax.nn.silu(condition).astype(BF16), ((0, 16 - count), (0, 0)))
    piece_b, piece_a = pack(where, w_qkv[0], w_proj[0], w_fc1[0], w_fc2[0], act_rows)
    stack_b = spread(piece_b)
    stack_a = spread(piece_a)

    bias_flat = jnp.zeros((8 * width,), F32)
    at = 0
    for own in (b_qv[0], b_proj[0], b_fc1[0], b_fc2[0]):
        bias_flat = lax.dynamic_update_slice(
            bias_flat, own.astype(F32), (at + place * own.shape[0],)
        )
        at += own.shape[0] * shards
    b_ada_row = lax.dynamic_update_slice(
        jnp.zeros((6 * width,), F32), b_ada[0].astype(F32), (place * b_ada.shape[1],)
    )[None]
    partial = modulate(where, stack_b, w_ada[0], b_ada_row, bias_flat.reshape(8, width))
    small = partial[0]
    for k in range(1, shards):
        small = small + xor_permute(partial[k], "fsdp", k)
    mod = small[:16].reshape(2, 8, width)
    bias = small[16:24]

    full_qkv, full_proj = assemble_b(where, *gathered(stack_b))
    full_fc1, full_fc2 = assemble_a(where, *gathered(stack_a))

    received = None
    for tick in range(sections):
        save = tick == sections - 1
        attn = run_attention_forward(
            where, latents, received, mod, bias, full_qkv, full_proj, save
        )
        feed = run_feed_forward(attn[0], mod, bias, full_fc1, full_fc2, save)
        if not save:
            received = lax.ppermute(
                feed[0], "section", [(i, i + 1) for i in range(sections - 1)]
            )
    middle, enter_one, triple, probs, heads_out, attended = attn
    section_out, enter_two, active, slope, projected = feed

    arrived = None
    last = sections - 1
    for tick in range(sections):
        save = tick == sections - 1
        back_feed = run_feed_backward(
            where, cotangent, arrived, middle, mod, full_fc1, full_fc2, slope, projected, last, save
        )
        if save:
            rows = (count * length, -1)
            send_a, keep_a = run_weights_a(
                where,
                shards,
                active.reshape(rows),
                back_feed[1].reshape(rows),
                enter_two.reshape(rows),
                back_feed[2].reshape(rows),
            )
            own_a, other_a = reduced(send_a, keep_a, place, side)
        back_attn = run_attention_backward(
            where,
            latents,
            received,
            back_feed[0],
            mod,
            full_qkv,
            full_proj,
            triple,
            probs,
            attended,
            save,
        )
        if not save:
            arrived = lax.ppermute(
                back_attn[0], "section", [(i + 1, i) for i in range(sections - 1)]
            )
    input_grads = back_attn[0]
    send_b, keep_b, aux = run_weights_b(
        where,
        shards,
        enter_one.reshape(rows),
        back_attn[2].reshape(rows),
        heads_out.reshape(rows),
        back_attn[1].reshape(rows),
        back_attn[3],
        back_feed[3],
        act_rows,
    )
    own_b, other_b = reduced(send_b, keep_b, place, side)

    aux_all = spread(aux)
    cond_parts = run_condition(where, aux_all, w_ada[0])
    cond_sum = cond_parts[0]
    for k in range(1, shards):
        cond_sum = cond_sum + xor_permute(cond_parts[k], "fsdp", k)
    for step in range(1, sections):
        moved = [(i, (i + step) % sections) for i in range(sections)]
        cond_total = lax.ppermute(cond_sum, "section", moved)
        cond_all = cond_total if step == 1 else cond_all + cond_total
    cond_all = cond_sum + cond_all
    gate = jax.nn.sigmoid(condition)
    cond_grad = cond_all * gate * (1.0 + condition * (1.0 - gate))

    bit = 2
    order = [2, 1]
    while 2 * bit < lax.axis_size("replica"):
        bit *= 2
        order.append(bit)
    for bit in order:
        aux_all = jnp.concatenate([aux_all, xor_permute(aux_all, "replica", bit)])
    grad_w_ada, sums = run_ada(where, aux_all, w_ada.shape[1])
    flat = sums.reshape(-1)

    def cut(offset, size):
        return lax.dynamic_slice(flat, (offset * width + place * size,), (size,))

    grad_qkv, grad_proj, grad_fc1, grad_fc2 = finish(where, own_a, other_a, own_b, other_b)
    outputs = (
        section_out,
        input_grads,
        grad_w_ada,
        cut(8, b_ada.shape[1]),
        grad_qkv,
        cut(0, b_qv.shape[1]),
        grad_proj,
        cut(2, b_proj.shape[1]),
        grad_fc1,
        cut(3, b_fc1.shape[1]),
        grad_fc2,
        cut(7, b_fc2.shape[1]),
    )
    outputs = [output[None] for output in outputs]
    return tuple(outputs[:2]) + (cond_grad,) + tuple(outputs[2:])


def solution(mesh):
    latent = P(("fsdp", "replica"), None, None)
    pair = P(("fsdp", "replica"), None)
    weight = P("section", "fsdp", None)
    bias = P("section", "fsdp")
    stacked = P("section", ("fsdp", "replica"), None, None)
    weights = (weight, bias) * 5
    return jax.shard_map(
        local,
        mesh=mesh,
        in_specs=(latent, pair, latent) + weights,
        out_specs=(stacked, stacked, pair) + weights,
        check_vma=False,
    )
```
